32 devices in a mesh: replica: 16 (over z, x, core), tensor: 2 (over y).
Axes of the slice: x: 2, y: 2, z: 4, core: 2. Of those that a mesh axis runs over, the one named last changes fastest.
Arguments:
- w_gate: bfloat16 [16, 1024, 3072], P('replica', None, 'tensor'), may hold values from -6 to 6
- w_up: bfloat16 [16, 1024, 3072], P('replica', None, 'tensor'), may hold values from -6 to 6
- w_down: bfloat16 [16, 3072, 1024], P('replica', 'tensor'), may hold values from -6 to 6
- pool: bfloat16 [16, 512, 1024], P('replica', None, 'tensor'), may hold values from -6 to 6
- rows_index: int32 [16, 2, 2, 128], P('replica'), may hold values from 0 to 511
- partners: int32 [2, 16], replicated, may hold values from 0 to 15, as said below
Outputs:
- new_gate: bfloat16 [16, 1024, 3072], P('replica', None, 'tensor')
- new_up: bfloat16 [16, 1024, 3072], P('replica', None, 'tensor')
- new_down: bfloat16 [16, 3072, 1024], P('replica', 'tensor')
The draws below stay inside these ranges and needn't reach their ends.
Inputs may be any that keep to these rules, and one draw needn't show every extreme that they name: Each row pairs the 16 replicas: partners[r, partners[r, i]] equals i and partners[r, i] differs from i.
All inputs are finite; a program needn't handle non-finite values.
Results may differ from the reference program's by a relative error of at most 0.029.
Values may be sent and summed in bfloat16 or wider, within the bound.
A program may use at most 128 MiB of HBM per device.

```python
import jax
import jax.numpy as jnp
from jax import lax

D = 1024
FF = 3072
ROWS = 128
ROUNDS = 2
POOL = 512
REPLICAS = 16
N_TENSOR = 2


def draw_partners(key, part):
    matchings = []
    for outer_step in range(ROUNDS):
        shuffled = jax.random.permutation(jax.random.fold_in(key, 17 + outer_step), REPLICAS).astype(jnp.int32)
        first_half = shuffled[0::2]
        second_half = shuffled[1::2]
        paired = jnp.zeros((REPLICAS,), jnp.int32).at[first_half].set(second_half).at[second_half].set(first_half)
        matchings.append(paired)
    return jnp.stack(matchings)


def with_ends(entries, key, smallest, top_value):
    longest = entries.shape.index(max(entries.shape))
    spots = []
    for shift in (0, 1):
        where = [jax.random.randint(jax.random.fold_in(key, axis), (), 0, length) for axis, length in enumerate(entries.shape)]
        where[longest] = (where[longest] + shift) % entries.shape[longest]
        spots.append(tuple(where))
    return entries.at[spots[0]].set(smallest).at[spots[1]].set(top_value)


def shard_levels(own_key, dims, cuts, smallest, largest):
    loudness = 1.0
    for dim, blocks in cuts:
        heights = jax.random.uniform(jax.random.fold_in(jax.random.fold_in(own_key, 6), dim), (blocks,), jnp.float32, smallest / len(cuts), largest / len(cuts))
        loudness = loudness * jnp.repeat(jnp.exp(heights), dims[dim] // blocks).reshape((-1,) + (1,) * (len(dims) - 1 - dim))
    return loudness


def noise(stream_key, dims, width, reach, cuts=(), kind=jnp.bfloat16):
    loudness = shard_levels(stream_key, dims, cuts, -0.22, 0.18) if cuts else 1.0
    result = jax.random.normal(stream_key, dims, jnp.float32) * width * loudness
    return jnp.minimum(jnp.maximum(result, -reach), reach).astype(kind)


def setup_inputs(seed: int = 0) -> dict:
    key_list = jax.random.split(jax.random.key(seed), 7)
    return {
        "w_gate": noise(key_list[0], (REPLICAS, D, FF), 1.0, 6.0, ((0, 16), (2, 2))),
        "w_up": noise(key_list[1], (REPLICAS, D, FF), 1.0, 6.0, ((0, 16), (2, 2))),
        "w_down": noise(key_list[2], (REPLICAS, FF, D), 1.0, 6.0, ((0, 16), (1, 2))),
        "pool": noise(key_list[3], (REPLICAS, POOL, D), 1.0, 6.0, ((0, 16), (2, 2))),
        "rows_index": with_ends(jax.random.randint(key_list[4], (REPLICAS, ROUNDS, 2, ROWS), 0, POOL), jax.random.fold_in(key_list[4], 1), 0, POOL - 1).astype(jnp.int32),
        "partners": draw_partners(jax.random.fold_in(key_list[6], 71), 0),
    }


inner_rate = 1.0
outer_rate = 0.5
momentum_rate = 0.9


def local_step(weights, pool_one, picked):
    w_gate, w_up, w_down = weights
    in_scale = D ** -0.5
    hid_scale = FF ** -0.5
    inputs = jnp.take(pool_one, picked[0].astype(jnp.int32), axis=0)
    targets = jnp.take(pool_one, picked[1].astype(jnp.int32), axis=0)
    gate_pre = jnp.dot(inputs, w_gate, preferred_element_type=jnp.float32) * in_scale
    up_value = jnp.dot(inputs, w_up, preferred_element_type=jnp.float32) * in_scale
    sigmoid_gate = jax.nn.sigmoid(gate_pre)
    active = gate_pre * sigmoid_gate
    hidden = (active * up_value).astype(jnp.bfloat16)
    grouped = hidden.reshape(ROWS, N_TENSOR, FF // N_TENSOR).astype(jnp.float32)
    down_groups = w_down.reshape(N_TENSOR, FF // N_TENSOR, D).astype(jnp.float32)
    group_terms = (jnp.einsum("rkf,kfd->krd", grouped, down_groups) * hid_scale).astype(jnp.bfloat16)
    branch = jnp.sum(group_terms.astype(jnp.float32), axis=0)
    errors = (inputs.astype(jnp.float32) + branch - targets.astype(jnp.float32)).astype(jnp.bfloat16)
    back_grad = jnp.dot(errors, w_down.T, preferred_element_type=jnp.float32) * hid_scale
    delta_gate = (back_grad * up_value * sigmoid_gate * (1.0 + gate_pre * (1.0 - sigmoid_gate))).astype(jnp.bfloat16)
    delta_up = (back_grad * active).astype(jnp.bfloat16)
    grad_gate = jnp.dot(inputs.T, delta_gate, preferred_element_type=jnp.float32) * in_scale
    grad_up = jnp.dot(inputs.T, delta_up, preferred_element_type=jnp.float32) * in_scale
    grad_down = jnp.dot(hidden.T, errors, preferred_element_type=jnp.float32) * hid_scale
    gradients = (grad_gate, grad_up, grad_down)
    return tuple((weight.astype(jnp.float32) - inner_rate * gradient).astype(jnp.bfloat16) for weight, gradient in zip(weights, gradients))


def outer_update(weight, stepped, partner_step, moment, partner_moment):
    pair_mean = 0.5 * (stepped.astype(jnp.float32) + partner_step.astype(jnp.float32))
    outer_grad = weight.astype(jnp.float32) - pair_mean
    moment_new = momentum_rate * 0.5 * (moment.astype(jnp.float32) + partner_moment.astype(jnp.float32)) + outer_grad
    updated = weight.astype(jnp.float32) - outer_rate * (momentum_rate * moment_new + outer_grad)
    return updated.astype(jnp.bfloat16), moment_new.astype(jnp.bfloat16)


def make_share(stepped, moment):
    return (0.475 * stepped.astype(jnp.float32) - 0.2025 * moment.astype(jnp.float32)).astype(jnp.bfloat16)


def final_update(weight, stepped, moment, partner_share):
    updated = 0.05 * weight.astype(jnp.float32) + 0.475 * stepped.astype(jnp.float32) - 0.2025 * moment.astype(jnp.float32) + partner_share.astype(jnp.float32)
    return updated.astype(jnp.bfloat16)


def reference(w_gate, w_up, w_down, pool, rows_index, partners):
    weights = (w_gate, w_up, w_down)
    moments = tuple(jnp.zeros_like(weight) for weight in weights)
    for outer_step in range(ROUNDS):
        def replica_step(operands):
            gate_one, up_one, down_one, pool_one, picked = operands
            return local_step((gate_one, up_one, down_one), pool_one, picked)

        stepped = lax.map(replica_step, (weights[0], weights[1], weights[2], pool, rows_index[:, outer_step]))
        partner_row = partners[outer_step]
        last_round = outer_step == ROUNDS - 1

        def replica_update(operands):
            replica_id, weight_set, moment_set, step_set = operands
            partner_id = partner_row[replica_id]
            new_weights = []
            new_moments = []
            for index_mat in range(3):
                if last_round:
                    partner_share = make_share(stepped[index_mat][partner_id], moments[index_mat][partner_id])
                    updated = final_update(weight_set[index_mat], step_set[index_mat], moment_set[index_mat], partner_share)
                    moment_new = moment_set[index_mat]
                else:
                    updated, moment_new = outer_update(weight_set[index_mat], step_set[index_mat], stepped[index_mat][partner_id], moment_set[index_mat], moments[index_mat][partner_id])
                new_weights.append(updated)
                new_moments.append(moment_new)
            return tuple(new_weights), tuple(new_moments)

        weights, moments = lax.map(replica_update, (jnp.arange(REPLICAS, dtype=jnp.int32), weights, moments, stepped))
    return weights[0], weights[1], weights[2]
```

```python
import jax
import jax.numpy as jnp
from jax import lax
from jax.sharding import PartitionSpec as P

ROUNDS = 2
inner_rate = 1.0
outer_rate = 0.5
momentum_rate = 0.9
AXES = ("replica", "tensor")
F32 = jnp.float32
BF16 = jnp.bfloat16


def bdot(a, b, ca, cb):
    return lax.dot_general(a, b, (((ca,), (cb,)), ((0,), (0,))), preferred_element_type=F32)


def local_step(weights, inputs, own_in, own_out, in_scale, hid_scale):
    w_gate, w_up, w_down = weights
    replicas, rows, dim = inputs.shape
    gate_pre = bdot(inputs, w_gate, 2, 2) * in_scale
    up_value = bdot(inputs, w_up, 2, 2) * in_scale
    sigmoid_gate = jax.nn.sigmoid(gate_pre)
    active = gate_pre * sigmoid_gate
    hidden = (active * up_value).astype(BF16)
    terms = (bdot(hidden, w_down, 2, 1) * hid_scale).astype(BF16)
    branch = lax.psum_scatter(
        terms.reshape(replicas * rows, dim), AXES, scatter_dimension=0, tiled=True
    ).astype(F32)
    own_err = (own_in.astype(F32) + branch - own_out.astype(F32)).astype(BF16)
    errors = lax.all_gather(own_err, AXES, axis=0, tiled=True).reshape(replicas, rows, dim)
    back_grad = bdot(errors, w_down, 2, 2) * hid_scale
    delta_gate = (
        back_grad * up_value * sigmoid_gate * (1.0 + gate_pre * (1.0 - sigmoid_gate))
    ).astype(BF16)
    delta_up = (back_grad * active).astype(BF16)
    grads = (
        bdot(delta_gate, inputs, 1, 1) * in_scale,
        bdot(delta_up, inputs, 1, 1) * in_scale,
        bdot(hidden, errors, 1, 1) * hid_scale,
    )
    return tuple((w.astype(F32) - inner_rate * g).astype(BF16) for w, g in zip(weights, grads))


def first_update(weight, stepped, partner):
    other = jnp.take(stepped, partner, axis=0)
    pair_mean = 0.5 * (stepped.astype(F32) + other.astype(F32))
    outer_grad = weight.astype(F32) - pair_mean
    updated = weight.astype(F32) - outer_rate * (momentum_rate * outer_grad + outer_grad)
    return updated.astype(BF16), outer_grad.astype(BF16)


def last_update(weight, stepped, moment, partner):
    own = 0.475 * stepped.astype(F32) - 0.2025 * moment.astype(F32)
    other = jnp.take(own.astype(BF16), partner, axis=0).astype(F32)
    return (0.05 * weight.astype(F32) + own + other).astype(BF16)


def body(w_gate, w_up, w_down, pool, rows_index, partners):
    nrep, nten = lax.axis_size("replica"), lax.axis_size("tensor")
    dim, units_home = w_gate.shape[1:]
    units = units_home // nrep
    in_scale, hid_scale = dim ** (-0.5), (units_home * nten) ** (-0.5)
    rows = rows_index.shape[3]

    def spread(w):
        return lax.all_to_all(w.reshape(nrep, units, dim), "replica", 0, 0, tiled=True)

    weights = (spread(w_gate[0].T), spread(w_up[0].T), spread(w_down[0]))

    picked = rows_index[0]
    in_cols = jnp.take(pool[0], picked[:, 0], axis=0)
    out_cols = jnp.take(pool[0], picked[:, 1], axis=0)
    t = lax.axis_index("tensor")
    own_rows = rows // nten
    full = lax.all_gather(in_cols, AXES, axis=0, tiled=False)
    full = full.reshape(nrep, nten, ROUNDS, rows, dim // nten)
    full = full.transpose(2, 0, 3, 1, 4).reshape(ROUNDS, nrep, rows, dim)
    targets = lax.all_gather(out_cols, "tensor", axis=2, tiled=True)
    own_out = lax.dynamic_slice_in_dim(targets, t * own_rows, own_rows, 1)
    own_in = lax.dynamic_index_in_dim(full, lax.axis_index("replica"), 1, keepdims=False)
    own_in = lax.dynamic_slice_in_dim(own_in, t * own_rows, own_rows, 1)

    moments = None
    for r in range(ROUNDS):
        stepped = local_step(weights, full[r], own_in[r], own_out[r], in_scale, hid_scale)
        if r < ROUNDS - 1:
            both = [first_update(w, s, partners[r]) for w, s in zip(weights, stepped)]
            weights = tuple(b[0] for b in both)
            moments = tuple(b[1] for b in both)
        else:
            weights = tuple(
                last_update(w, s, m, partners[r]) for w, s, m in zip(weights, stepped, moments)
            )

    def home(w):
        return lax.all_to_all(w, "replica", 0, 0, tiled=True).reshape(units_home, dim)

    return (home(weights[0]).T[None], home(weights[1]).T[None], home(weights[2])[None])


def solution(mesh):
    return jax.shard_map(
        body,
        mesh=mesh,
        in_specs=(
            P("replica", None, "tensor"),
            P("replica", None, "tensor"),
            P("replica", "tensor", None),
            P("replica", None, "tensor"),
            P("replica", None, None, None),
            P(),
        ),
        out_specs=(
            P("replica", None, "tensor"),
            P("replica", None, "tensor"),
            P("replica", "tensor", None),
        ),
        check_vma=False,
    )
```

```python
import functools

import jax
import jax.numpy as jnp
from jax import lax
from jax.experimental import pallas as pl
from jax.experimental.pallas import tpu as pltpu
from jax.sharding import PartitionSpec as P

ROUNDS = 2
inner_rate = 1.0
outer_rate = 0.5
momentum_rate = 0.9
AXES = ("replica", "tensor")
F32 = jnp.float32
BF16 = jnp.bfloat16


def bdot(a, b, ca, cb):
    return lax.dot_general(a, b, (((ca,), (cb,)), ((0,), (0,))), preferred_element_type=F32)


def home_step(weights, inputs, targets, in_scale, hid_scale):
    w_gate, w_up, w_down = weights
    rows_last = (((1,), (1,)), ((), ()))
    gate_pre = lax.dot_general(w_gate, inputs, rows_last, preferred_element_type=F32) * in_scale
    up_value = lax.dot_general(w_up, inputs, rows_last, preferred_element_type=F32) * in_scale
    sigmoid_gate = jax.nn.sigmoid(gate_pre)
    active = gate_pre * sigmoid_gate
    hidden = (active * up_value).astype(BF16)
    term = lax.dot_general(
        hidden, w_down, (((0,), (0,)), ((), ())), preferred_element_type=F32
    ) * hid_scale
    branch = lax.psum(term.astype(BF16), "tensor").astype(F32)
    errors = (inputs.astype(F32) + branch - targets.astype(F32)).astype(BF16)
    back = lax.dot_general(w_down, errors, rows_last, preferred_element_type=F32) * hid_scale
    delta_gate = (
        back * up_value * sigmoid_gate * (1.0 + gate_pre * (1.0 - sigmoid_gate))
    ).astype(BF16)
    delta_up = (back * active).astype(BF16)
    return (delta_gate, delta_up, hidden), errors


def flip(index, bit):
    return index + bit * (1 - 2 * ((index // bit) % 2))


def exchange_kernel(plans, nrep, nten, terms, own_in, own_out, out, *scratch):
    nbits = len(plans[0][1])
    nplan = len(plans)
    tbits = nten.bit_length() - 1
    bufs, (send_sem, recv_sem) = scratch[: -2], scratch[-2:]
    rep, ten = lax.axis_index("replica"), lax.axis_index("tensor")

    def bit_of(k):
        return (ten // (1 << k)) % 2 if k < tbits else (rep // (1 << (k - tbits))) % 2

    def peer(k):
        if k < tbits:
            return (rep, flip(ten, 1 << k))
        return (flip(rep, 1 << (k - tbits)), ten)

    barrier = pltpu.get_barrier_semaphore()
    for k in range(nbits):
        pl.semaphore_signal(
            barrier, inc=1, device_id=peer(k), device_id_type=pl.DeviceIdType.MESH
        )
    pl.semaphore_wait(barrier, nbits)

    state = []
    for index, (cols, order) in enumerate(plans):
        state.append(dict(cols=cols, order=order, left=list(range(nbits))[::-1], cur=terms, own=True))

    def start_half(p, s):
        st = state[p]
        k = st["order"][s]
        pos = st["left"].index(k)
        keep, give = [slice(None)] * len(st["left"]), [slice(None)] * len(st["left"])
        keep[pos], give[pos] = bit_of(k), 1 - bit_of(k)
        tail = (slice(None), pl.ds(st["cols"][0], st["cols"][1])) if st["own"] else (slice(None), slice(None))
        buf = bufs[p * nbits + s]
        copy = pltpu.make_async_remote_copy(
            src_ref=st["cur"].at[tuple(give) + tail],
            dst_ref=buf,
            send_sem=send_sem.at[p, s],
            recv_sem=recv_sem.at[p, s],
            device_id=peer(k),
            device_id_type=pl.DeviceIdType.MESH,
        )
        copy.start()
        st.update(copy=copy, pos=pos, tail=tail, buf=buf)

    def end_half(p, s):
        st = state[p]
        st["copy"].wait()
        rest = len(st["left"]) - 1
        k = st["order"][s]
        for flat in range(1 << rest):
            bits = [(flat >> (rest - 1 - i)) & 1 for i in range(rest)]
            src = bits[: st["pos"]] + [bit_of(k)] + bits[st["pos"] :]
            mine = st["cur"][tuple(src) + st["tail"]].astype(F32)
            dst = tuple(bits) + (slice(None), slice(None))
            st["buf"][dst] = (mine + st["buf"][dst].astype(F32)).astype(BF16)
        st["left"].remove(k)
        st.update(cur=st["buf"], own=False)

    for p in range(nplan):
        start_half(p, 0)
    for s in range(nbits):
        for p in range(nplan):
            end_half(p, s)
            if s + 1 < nbits:
                start_half(p, s + 1)

    def held(p, s):
        fixed = state[p]["order"][: s + 1]
        lead = [bit_of(k) if k in fixed else slice(None) for k in range(nbits)[::-1]]
        return tuple(lead) + (slice(None), pl.ds(state[p]["cols"][0], state[p]["cols"][1]))

    def start_double(p, s):
        k = state[p]["order"][s]
        where = held(p, s)
        copy = pltpu.make_async_remote_copy(
            src_ref=out.at[where],
            dst_ref=out.at[where],
            send_sem=send_sem.at[p, nbits + s],
            recv_sem=recv_sem.at[p, nbits + s],
            device_id=peer(k),
            device_id_type=pl.DeviceIdType.MESH,
        )
        copy.start()
        state[p]["copy"] = copy

    for p in range(nplan):
        first, count = state[p]["cols"]
        sl = (slice(None), pl.ds(first, count))
        error = own_in[sl].astype(F32) + state[p]["buf"][...].astype(F32) - own_out[sl].astype(F32)
        out[held(p, nbits - 1)] = error.astype(BF16)
        start_double(p, nbits - 1)
    for s in range(nbits)[::-1]:
        for p in range(nplan):
            state[p]["copy"].wait()
            if s > 0:
                start_double(p, s - 1)


def exchange(terms, own_in, own_out, nrep, nten):
    rows, dim = own_in.shape
    nbits = (nrep * nten).bit_length() - 1
    tbits = nten.bit_length() - 1
    ring = list(range(tbits)) + list(range(tbits + 1, nbits))
    half = dim // 2
    orders = ([tbits] + ring, [tbits] + ring[tbits:] + ring[:tbits])
    plans = [((i * half, half), orders[i]) for i in range(2)]
    view = (2,) * nbits + (rows, dim)
    scratch = [
        pltpu.VMEM((2,) * (nbits - 1 - s) + (rows, half), BF16) for _ in plans for s in range(nbits)
    ]
    scratch += [pltpu.SemaphoreType.DMA((2, 2 * nbits))] * 2
    vmem = pl.BlockSpec(memory_space=pltpu.VMEM)
    out = pl.pallas_call(
        functools.partial(exchange_kernel, plans, nrep, nten),
        out_shape=jax.ShapeDtypeStruct(view, BF16),
        in_specs=[vmem] * 3,
        out_specs=vmem,
        scratch_shapes=scratch,
        compiler_params=pltpu.CompilerParams(
            collective_id=0, has_side_effects=True, vmem_limit_bytes=62 << 20
        ),
    )(terms.reshape(view), own_in, own_out)
    return out.reshape(nrep, nten * rows, dim)


def slice_step(weights, inputs, own_in, own_out, in_scale, hid_scale):
    w_gate, w_up, w_down = weights
    replicas, rows, dim = inputs.shape
    gate_pre = bdot(inputs, w_gate, 2, 2) * in_scale
    up_value = bdot(inputs, w_up, 2, 2) * in_scale
    sigmoid_gate = jax.nn.sigmoid(gate_pre)
    active = gate_pre * sigmoid_gate
    hidden = (active * up_value).astype(BF16)
    terms = (bdot(hidden, w_down, 2, 1) * hid_scale).astype(BF16)
    nrep, nten = lax.axis_size("replica"), lax.axis_size("tensor")
    total = nrep * nten
    if total & (total - 1) == 0 and total * own_in.size <= 1 << 22:
        errors = exchange(terms, own_in, own_out, nrep, nten)
    else:
        branch = lax.psum_scatter(
            terms.reshape(replicas * rows, dim), AXES, scatter_dimension=0, tiled=True
        ).astype(F32)
        own_err = (own_in.astype(F32) + branch - own_out.astype(F32)).astype(BF16)
        errors = lax.all_gather(own_err, AXES, axis=0, tiled=True).reshape(replicas, rows, dim)
    back_grad = bdot(errors, w_down, 2, 2) * hid_scale
    delta_gate = (
        back_grad * up_value * sigmoid_gate * (1.0 + gate_pre * (1.0 - sigmoid_gate))
    ).astype(BF16)
    delta_up = (back_grad * active).astype(BF16)
    grads = (
        bdot(delta_gate, inputs, 1, 1) * in_scale,
        bdot(delta_up, inputs, 1, 1) * in_scale,
        bdot(hidden, errors, 1, 1) * hid_scale,
    )
    return tuple((w.astype(F32) - inner_rate * g).astype(BF16) for w, g in zip(weights, grads))


def first_update(weight, stepped, partner):
    other = jnp.take(stepped, partner, axis=0)
    pair_mean = 0.5 * (stepped.astype(F32) + other.astype(F32))
    outer_grad = weight.astype(F32) - pair_mean
    updated = weight.astype(F32) - outer_rate * (momentum_rate * outer_grad + outer_grad)
    return updated.astype(BF16), outer_grad.astype(BF16)


def last_update(weight, stepped, moment, partner):
    own = 0.475 * stepped.astype(F32) - 0.2025 * moment.astype(F32)
    other = jnp.take(own.astype(BF16), partner, axis=0).astype(F32)
    return (0.05 * weight.astype(F32) + own + other).astype(BF16)


def body(w_gate, w_up, w_down, pool, rows_index, partners):
    nrep, nten = lax.axis_size("replica"), lax.axis_size("tensor")
    dim, units_home = w_gate.shape[1:]
    units = units_home // nrep
    in_scale, hid_scale = dim ** (-0.5), (units_home * nten) ** (-0.5)
    rows = rows_index.shape[3]

    def spread(w):
        return lax.all_to_all(w.reshape(nrep, units, dim), "replica", 0, 0, tiled=True)

    at_home = (w_gate[0].T, w_up[0].T, w_down[0])
    weights = tuple(spread(w) for w in at_home)

    picked = rows_index[0]
    in_cols = jnp.take(pool[0], picked[:, 0], axis=0)
    out_cols = jnp.take(pool[0], picked[:, 1], axis=0)
    r, t = lax.axis_index("replica"), lax.axis_index("tensor")
    own_rows = rows // nten

    def mine(x, axis):
        return lax.dynamic_slice_in_dim(x, t * own_rows, own_rows, axis)

    both = lax.all_gather(jnp.stack([in_cols, out_cols]), "tensor", axis=3, tiled=True)
    inputs, targets = both[0], both[1]
    factors, errors = home_step(at_home, inputs[0], targets[0], in_scale, hid_scale)
    full = lax.all_gather(mine(inputs, 1), AXES, axis=0, tiled=False)
    full = full.transpose(1, 0, 2, 3).reshape(ROUNDS, nrep, rows, dim)
    all_errors = lax.all_gather(mine(errors, 0), AXES, axis=0, tiled=True).reshape(nrep, rows, dim)
    stacked = jnp.stack([f.reshape(nrep, units, rows) for f in factors], axis=1)
    factors = lax.all_to_all(stacked, "replica", 0, 0, tiled=True)

    sides = (full[0], full[0], all_errors)
    scales = (in_scale, in_scale, hid_scale)
    moments = []
    updated = []
    for i in range(3):
        grad = bdot(factors[:, i], sides[i], 2, 1) * scales[i]
        stepped = (weights[i].astype(F32) - inner_rate * grad).astype(BF16)
        pair = first_update(weights[i], stepped, partners[0])
        updated.append(pair[0])
        moments.append(pair[1])
    stepped = slice_step(
        tuple(updated), full[1], mine(inputs[1], 0), mine(targets[1], 0), in_scale, hid_scale
    )
    weights = tuple(last_update(w, s, m, partners[1]) for w, s, m in zip(updated, stepped, moments))

    def home(w):
        return lax.all_to_all(w, "replica", 0, 0, tiled=True).reshape(units_home, dim)

    return (home(weights[0]).T[None], home(weights[1]).T[None], home(weights[2])[None])


def solution(mesh):
    return jax.shard_map(
        body,
        mesh=mesh,
        in_specs=(
            P("replica", None, "tensor"),
            P("replica", None, "tensor"),
            P("replica", "tensor", None),
            P("replica", None, "tensor"),
            P("replica", None, None, None),
            P(),
        ),
        out_specs=(
            P("replica", None, "tensor"),
            P("replica", None, "tensor"),
            P("replica", "tensor", None),
        ),
        check_vma=False,
    )
```

```python
import functools

import jax
import jax.numpy as jnp
from jax import lax
from jax.experimental import pallas as pl
from jax.experimental.pallas import tpu as pltpu
from jax.sharding import PartitionSpec as P

ROUNDS = 2
inner_rate = 1.0
outer_rate = 0.5
momentum_rate = 0.9
AXES = ("replica", "tensor")
F32 = jnp.float32
BF16 = jnp.bfloat16


def bdot(a, b, ca, cb):
    return lax.dot_general(a, b, (((ca,), (cb,)), ((0,), (0,))), preferred_element_type=F32)


def home_step(weights, inputs, targets, in_scale, hid_scale):
    w_gate, w_up, w_down = weights
    rows_last = (((1,), (1,)), ((), ()))
    gate_pre = lax.dot_general(w_gate, inputs, rows_last, preferred_element_type=F32) * in_scale
    up_value = lax.dot_general(w_up, inputs, rows_last, preferred_element_type=F32) * in_scale
    sigmoid_gate = jax.nn.sigmoid(gate_pre)
    active = gate_pre * sigmoid_gate
    hidden = (active * up_value).astype(BF16)
    term = lax.dot_general(
        hidden, w_down, (((0,), (0,)), ((), ())), preferred_element_type=F32
    ) * hid_scale
    branch = lax.psum(term.astype(BF16), "tensor").astype(F32)
    errors = (inputs.astype(F32) + branch - targets.astype(F32)).astype(BF16)
    back = lax.dot_general(w_down, errors, rows_last, preferred_element_type=F32) * hid_scale
    delta_gate = (
        back * up_value * sigmoid_gate * (1.0 + gate_pre * (1.0 - sigmoid_gate))
    ).astype(BF16)
    delta_up = (back * active).astype(BF16)
    return (delta_gate, delta_up, hidden), errors


def flip(index, bit):
    return index + bit * (1 - 2 * ((index // bit) % 2))


def exchange_kernel(plans, nrep, nten, terms, own_in, own_out, out, *scratch):
    nbits = len(plans[0][1])
    nplan = len(plans)
    tbits = nten.bit_length() - 1
    bufs, (send_sem, recv_sem) = scratch[: -2], scratch[-2:]
    rep, ten = lax.axis_index("replica"), lax.axis_index("tensor")

    def bit_of(k):
        return (ten // (1 << k)) % 2 if k < tbits else (rep // (1 << (k - tbits))) % 2

    def peer(k):
        if k < tbits:
            return (rep, flip(ten, 1 << k))
        return (flip(rep, 1 << (k - tbits)), ten)

    barrier = pltpu.get_barrier_semaphore()
    for k in range(nbits):
        pl.semaphore_signal(
            barrier, inc=1, device_id=peer(k), device_id_type=pl.DeviceIdType.MESH
        )
    pl.semaphore_wait(barrier, nbits)

    state = []
    for index, (cols, order) in enumerate(plans):
        state.append(dict(cols=cols, order=order, left=list(range(nbits))[::-1], cur=terms, own=True))

    def start_half(p, s):
        st = state[p]
        k = st["order"][s]
        pos = st["left"].index(k)
        keep, give = [slice(None)] * len(st["left"]), [slice(None)] * len(st["left"])
        keep[pos], give[pos] = bit_of(k), 1 - bit_of(k)
        tail = (slice(None), pl.ds(st["cols"][0], st["cols"][1])) if st["own"] else (slice(None), slice(None))
        buf = bufs[p * nbits + s]
        copy = pltpu.make_async_remote_copy(
            src_ref=st["cur"].at[tuple(give) + tail],
            dst_ref=buf,
            send_sem=send_sem.at[p, s],
            recv_sem=recv_sem.at[p, s],
            device_id=peer(k),
            device_id_type=pl.DeviceIdType.MESH,
        )
        copy.start()
        st.update(copy=copy, pos=pos, tail=tail, buf=buf)

    def end_half(p, s):
        st = state[p]
        st["copy"].wait()
        rest = len(st["left"]) - 1
        k = st["order"][s]
        for flat in range(1 << rest):
            bits = [(flat >> (rest - 1 - i)) & 1 for i in range(rest)]
            src = bits[: st["pos"]] + [bit_of(k)] + bits[st["pos"] :]
            mine = st["cur"][tuple(src) + st["tail"]].astype(F32)
            dst = tuple(bits) + (slice(None), slice(None))
            st["buf"][dst] = (mine + st["buf"][dst].astype(F32)).astype(BF16)
        st["left"].remove(k)
        st.update(cur=st["buf"], own=False)

    for p in range(nplan):
        start_half(p, 0)
    for s in range(nbits):
        for p in range(nplan):
            end_half(p, s)
            if s + 1 < nbits:
                start_half(p, s + 1)

    def held(p, s):
        fixed = state[p]["order"][: s + 1]
        lead = [bit_of(k) if k in fixed else slice(None) for k in range(nbits)[::-1]]
        return tuple(lead) + (slice(None), pl.ds(state[p]["cols"][0], state[p]["cols"][1]))

    def start_double(p, s):
        k = state[p]["order"][s]
        where = held(p, s)
        copy = pltpu.make_async_remote_copy(
            src_ref=out.at[where],
            dst_ref=out.at[where],
            send_sem=send_sem.at[p, nbits + s],
            recv_sem=recv_sem.at[p, nbits + s],
            device_id=peer(k),
            device_id_type=pl.DeviceIdType.MESH,
        )
        copy.start()
        state[p]["copy"] = copy

    for p in range(nplan):
        first, count = state[p]["cols"]
        sl = (slice(None), pl.ds(first, count))
        error = own_in[sl].astype(F32) + state[p]["buf"][...].astype(F32) - own_out[sl].astype(F32)
        out[held(p, nbits - 1)] = error.astype(BF16)
        start_double(p, nbits - 1)
    for s in range(nbits)[::-1]:
        for p in range(nplan):
            state[p]["copy"].wait()
            if s > 0:
                start_double(p, s - 1)


def exchange(terms, own_in, own_out, nrep, nten):
    rows, dim = own_in.shape
    nbits = (nrep * nten).bit_length() - 1
    tbits = nten.bit_length() - 1
    ring = list(range(tbits)) + list(range(tbits + 1, nbits))
    half = dim // 2
    orders = ([tbits] + ring, [tbits] + ring[tbits:] + ring[:tbits])
    plans = [((i * half, half), orders[i]) for i in range(2)]
    view = (2,) * nbits + (rows, dim)
    scratch = [
        pltpu.VMEM((2,) * (nbits - 1 - s) + (rows, half), BF16) for _ in plans for s in range(nbits)
    ]
    scratch += [pltpu.SemaphoreType.DMA((2, 2 * nbits))] * 2
    vmem = pl.BlockSpec(memory_space=pltpu.VMEM)
    out = pl.pallas_call(
        functools.partial(exchange_kernel, plans, nrep, nten),
        out_shape=jax.ShapeDtypeStruct(view, BF16),
        in_specs=[vmem] * 3,
        out_specs=vmem,
        scratch_shapes=scratch,
        compiler_params=pltpu.CompilerParams(
            collective_id=0, has_side_effects=True, vmem_limit_bytes=62 << 20
        ),
    )(terms.reshape(view), own_in, own_out)
    return out.reshape(nrep, nten * rows, dim)


def dot_in(a, b):
    return lax.dot_general(a, b, (((1,), (1,)), ((), ())), preferred_element_type=F32)


def update_kernel(scales, partner, *refs):
    own, other = refs[:6], refs[6:12]
    x2 = refs[12]
    new_w, new_m = refs[13:16], refs[16:19]
    pre, hid, terms = refs[19:22]
    in_scale, hid_scale = scales

    def stepped(group, i, scale):
        weight, fac, side = group[i][0], group[3][0, i], group[5 if i == 2 else 4][0]
        grad = jnp.dot(fac, side, preferred_element_type=F32) * scale
        return (weight.astype(F32) - inner_rate * grad).astype(BF16).astype(F32)

    for i in range(3):
        scale = hid_scale if i == 2 else in_scale
        pair_mean = 0.5 * (stepped(own, i, scale) + stepped(other, i, scale))
        weight = own[i][0].astype(F32)
        outer_grad = weight - pair_mean
        updated = weight - outer_rate * (momentum_rate * outer_grad + outer_grad)
        new_w[i][0] = updated.astype(BF16)
        new_m[i][0] = outer_grad.astype(BF16)
    gate_pre = dot_in(new_w[0][0], x2[0]) * in_scale
    up_value = dot_in(new_w[1][0], x2[0]) * in_scale
    hidden = (gate_pre * jax.nn.sigmoid(gate_pre) * up_value).astype(BF16)
    term = lax.dot_general(
        hidden, new_w[2][0], (((0,), (0,)), ((), ())), preferred_element_type=F32
    ) * hid_scale
    pre[0, 0] = gate_pre
    pre[0, 1] = up_value
    hid[0] = hidden
    terms[0] = term.astype(BF16)


def last_kernel(scales, partner, *refs):
    own, other, outs = refs[:10], refs[10:20], refs[20:]
    in_scale, hid_scale = scales

    def shares(group):
        x2, e2, pre, hid = group[6][0], group[7][0], group[8], group[9][0]
        gate_pre, up_value = pre[0, 0], pre[0, 1]
        back = dot_in(group[2][0], e2) * hid_scale
        sig = jax.nn.sigmoid(gate_pre)
        delta_gate = (back * up_value * sig * (1.0 + gate_pre * (1.0 - sig))).astype(BF16)
        delta_up = (back * (gate_pre * sig)).astype(BF16)
        for i, (fac, side, scale) in enumerate(
            ((delta_gate, x2, in_scale), (delta_up, x2, in_scale), (hid, e2, hid_scale))
        ):
            grad = jnp.dot(fac, side, preferred_element_type=F32) * scale
            local = (group[i][0].astype(F32) - inner_rate * grad).astype(BF16).astype(F32)
            yield 0.475 * local - 0.2025 * group[3 + i][0].astype(F32)

    for i, (mine, theirs) in enumerate(zip(shares(own), shares(other))):
        total = 0.05 * own[i][0].astype(F32) + mine + theirs.astype(BF16).astype(F32)
        outs[i][0] = total.astype(BF16)


def over_replicas(kernel, scales, partner, paired, single, out_shapes, flops):
    nrep = partner.shape[0]

    def spec(shape, swap):
        zeros = (0,) * (len(shape) - 1)
        if swap:
            return pl.BlockSpec((1,) + shape[1:], lambda p, who: (who[p],) + zeros)
        return pl.BlockSpec((1,) + shape[1:], lambda p, who: (p,) + zeros)

    args = list(paired) + list(paired) + list(single)
    swaps = [False] * len(paired) + [True] * len(paired) + [False] * len(single)
    moved = sum(a.size * a.dtype.itemsize for a in args)
    return pl.pallas_call(
        functools.partial(kernel, scales),
        grid_spec=pltpu.PrefetchScalarGridSpec(
            num_scalar_prefetch=1,
            grid=(nrep,),
            in_specs=[spec(a.shape, w) for a, w in zip(args, swaps)],
            out_specs=[spec(o.shape, False) for o in out_shapes],
        ),
        out_shape=out_shapes,
        cost_estimate=pl.CostEstimate(flops=flops, bytes_accessed=moved, transcendentals=0),
        compiler_params=pltpu.CompilerParams(vmem_limit_bytes=40 << 20),
    )(partner, *args)


def rounds_in_kernels(weights, factors, x1, e1, x2, own_in, own_out, partners, scales):
    nrep, units, dim = weights[0].shape
    nten = lax.axis_size("tensor")
    rows = x1.shape[1]
    like = jax.ShapeDtypeStruct((nrep, units, dim), BF16)
    flops = 18 * nrep * units * rows * dim
    res = over_replicas(
        update_kernel,
        scales,
        partners[0],
        list(weights) + [factors, x1, e1],
        [x2],
        [like] * 6
        + [
            jax.ShapeDtypeStruct((nrep, 2, units, rows), F32),
            jax.ShapeDtypeStruct((nrep, units, rows), BF16),
            jax.ShapeDtypeStruct((nrep, rows, dim), BF16),
        ],
        flops,
    )
    pre, hid, terms = res[6:]
    e2 = exchange(terms, own_in, own_out, nrep, nten)
    return over_replicas(
        last_kernel, scales, partners[1], list(res[:6]) + [x2, e2, pre, hid], [], [like] * 3, flops
    )


def slice_step(weights, inputs, own_in, own_out, in_scale, hid_scale):
    w_gate, w_up, w_down = weights
    replicas, rows, dim = inputs.shape
    gate_pre = bdot(inputs, w_gate, 2, 2) * in_scale
    up_value = bdot(inputs, w_up, 2, 2) * in_scale
    sigmoid_gate = jax.nn.sigmoid(gate_pre)
    active = gate_pre * sigmoid_gate
    hidden = (active * up_value).astype(BF16)
    terms = (bdot(hidden, w_down, 2, 1) * hid_scale).astype(BF16)
    branch = lax.psum_scatter(
        terms.reshape(replicas * rows, dim), AXES, scatter_dimension=0, tiled=True
    ).astype(F32)
    own_err = (own_in.astype(F32) + branch - own_out.astype(F32)).astype(BF16)
    errors = lax.all_gather(own_err, AXES, axis=0, tiled=True).reshape(replicas, rows, dim)
    back_grad = bdot(errors, w_down, 2, 2) * hid_scale
    delta_gate = (
        back_grad * up_value * sigmoid_gate * (1.0 + gate_pre * (1.0 - sigmoid_gate))
    ).astype(BF16)
    delta_up = (back_grad * active).astype(BF16)
    grads = (
        bdot(delta_gate, inputs, 1, 1) * in_scale,
        bdot(delta_up, inputs, 1, 1) * in_scale,
        bdot(hidden, errors, 1, 1) * hid_scale,
    )
    return tuple((w.astype(F32) - inner_rate * g).astype(BF16) for w, g in zip(weights, grads))


def first_update(weight, stepped, partner):
    other = jnp.take(stepped, partner, axis=0)
    pair_mean = 0.5 * (stepped.astype(F32) + other.astype(F32))
    outer_grad = weight.astype(F32) - pair_mean
    updated = weight.astype(F32) - outer_rate * (momentum_rate * outer_grad + outer_grad)
    return updated.astype(BF16), outer_grad.astype(BF16)


def last_update(weight, stepped, moment, partner):
    own = 0.475 * stepped.astype(F32) - 0.2025 * moment.astype(F32)
    other = jnp.take(own.astype(BF16), partner, axis=0).astype(F32)
    return (0.05 * weight.astype(F32) + own + other).astype(BF16)


def body(w_gate, w_up, w_down, pool, rows_index, partners):
    nrep, nten = lax.axis_size("replica"), lax.axis_size("tensor")
    dim, units_home = w_gate.shape[1:]
    units = units_home // nrep
    in_scale, hid_scale = dim ** (-0.5), (units_home * nten) ** (-0.5)
    rows = rows_index.shape[3]

    def spread(w):
        return lax.all_to_all(w.reshape(nrep, units, dim), "replica", 0, 0, tiled=True)

    at_home = (w_gate[0].T, w_up[0].T, w_down[0])
    weights = tuple(spread(w) for w in at_home)

    picked = rows_index[0]
    in_cols = jnp.take(pool[0], picked[:, 0], axis=0)
    out_cols = jnp.take(pool[0], picked[:, 1], axis=0)
    r, t = lax.axis_index("replica"), lax.axis_index("tensor")
    own_rows = rows // nten

    def mine(x, axis):
        return lax.dynamic_slice_in_dim(x, t * own_rows, own_rows, axis)

    both = lax.all_gather(jnp.stack([in_cols, out_cols]), "tensor", axis=3, tiled=True)
    inputs, targets = both[0], both[1]
    factors, errors = home_step(at_home, inputs[0], targets[0], in_scale, hid_scale)
    full = lax.all_gather(mine(inputs, 1), AXES, axis=0, tiled=False)
    full = full.transpose(1, 0, 2, 3).reshape(ROUNDS, nrep, rows, dim)
    all_errors = lax.all_gather(mine(errors, 0), AXES, axis=0, tiled=True).reshape(nrep, rows, dim)
    stacked = jnp.stack([f.reshape(nrep, units, rows) for f in factors], axis=1)
    weights, stacked = lax.optimization_barrier((weights, stacked))
    factors = lax.all_to_all(stacked, "replica", 0, 0, tiled=True)
    own_in, own_out = mine(inputs[1], 0), mine(targets[1], 0)

    total = nrep * nten
    if units % 16 == 0 and total & (total - 1) == 0 and total * own_in.size <= 1 << 22:
        weights = rounds_in_kernels(
            weights, factors, full[0], all_errors, full[1], own_in, own_out, partners,
            (in_scale, hid_scale),
        )
    else:
        sides = (full[0], full[0], all_errors)
        scales = (in_scale, in_scale, hid_scale)
        moments = []
        updated = []
        for i in range(3):
            grad = bdot(factors[:, i], sides[i], 2, 1) * scales[i]
            stepped = (weights[i].astype(F32) - inner_rate * grad).astype(BF16)
            pair = first_update(weights[i], stepped, partners[0])
            updated.append(pair[0])
            moments.append(pair[1])
        stepped = slice_step(tuple(updated), full[1], own_in, own_out, in_scale, hid_scale)
        weights = tuple(
            last_update(w, s, m, partners[1]) for w, s, m in zip(updated, stepped, moments)
        )

    def home(w):
        return lax.all_to_all(w, "replica", 0, 0, tiled=True).reshape(units_home, dim)

    return (home(weights[0]).T[None], home(weights[1]).T[None], home(weights[2])[None])


def solution(mesh):
    return jax.shard_map(
        body,
        mesh=mesh,
        in_specs=(
            P("replica", None, "tensor"),
            P("replica", None, "tensor"),
            P("replica", "tensor", None),
            P("replica", None, "tensor"),
            P("replica", None, None, None),
            P(),
        ),
        out_specs=(
            P("replica", None, "tensor"),
            P("replica", None, "tensor"),
            P("replica", "tensor", None),
        ),
        check_vma=False,
    )
```

```python
import functools

import jax
import jax.numpy as jnp
from jax import lax
from jax.experimental import pallas as pl
from jax.experimental.pallas import tpu as pltpu
from jax.sharding import PartitionSpec as P

ROUNDS = 2
inner_rate = 1.0
outer_rate = 0.5
momentum_rate = 0.9
AXES = ("replica", "tensor")
F32 = jnp.float32
BF16 = jnp.bfloat16


def bdot(a, b, ca, cb):
    return lax.dot_general(a, b, (((ca,), (cb,)), ((0,), (0,))), preferred_element_type=F32)


def home_step(weights, inputs, targets, in_scale, hid_scale):
    w_gate, w_up, w_down = weights
    rows_last = (((1,), (1,)), ((), ()))
    gate_pre = lax.dot_general(w_gate, inputs, rows_last, preferred_element_type=F32) * in_scale
    up_value = lax.dot_general(w_up, inputs, rows_last, preferred_element_type=F32) * in_scale
    sigmoid_gate = jax.nn.sigmoid(gate_pre)
    active = gate_pre * sigmoid_gate
    hidden = (active * up_value).astype(BF16)
    term = lax.dot_general(
        hidden, w_down, (((0,), (0,)), ((), ())), preferred_element_type=F32
    ) * hid_scale
    branch = lax.psum(term.astype(BF16), "tensor").astype(F32)
    errors = (inputs.astype(F32) + branch - targets.astype(F32)).astype(BF16)
    back = lax.dot_general(w_down, errors, rows_last, preferred_element_type=F32) * hid_scale
    delta_gate = (
        back * up_value * sigmoid_gate * (1.0 + gate_pre * (1.0 - sigmoid_gate))
    ).astype(BF16)
    delta_up = (back * active).astype(BF16)
    return (delta_gate, delta_up, hidden), errors


def flip(index, bit):
    return index + bit * (1 - 2 * ((index // bit) % 2))


def exchange_kernel(plans, nrep, nten, terms, own_in, own_out, out, *scratch):
    nbits = len(plans[0][1])
    nplan = len(plans)
    tbits = nten.bit_length() - 1
    bufs, (send_sem, recv_sem) = scratch[: -2], scratch[-2:]
    rep, ten = lax.axis_index("replica"), lax.axis_index("tensor")

    def bit_of(k):
        return (ten // (1 << k)) % 2 if k < tbits else (rep // (1 << (k - tbits))) % 2

    def peer(k):
        if k < tbits:
            return (rep, flip(ten, 1 << k))
        return (flip(rep, 1 << (k - tbits)), ten)

    barrier = pltpu.get_barrier_semaphore()
    for k in range(nbits):
        pl.semaphore_signal(
            barrier, inc=1, device_id=peer(k), device_id_type=pl.DeviceIdType.MESH
        )
    pl.semaphore_wait(barrier, nbits)

    state = []
    for index, (cols, order) in enumerate(plans):
        state.append(dict(cols=cols, order=order, left=list(range(nbits))[::-1], cur=terms, own=True))

    def start_half(p, s):
        st = state[p]
        k = st["order"][s]
        pos = st["left"].index(k)
        keep, give = [slice(None)] * len(st["left"]), [slice(None)] * len(st["left"])
        keep[pos], give[pos] = bit_of(k), 1 - bit_of(k)
        tail = (slice(None), pl.ds(st["cols"][0], st["cols"][1])) if st["own"] else (slice(None), slice(None))
        buf = bufs[p * nbits + s]
        copy = pltpu.make_async_remote_copy(
            src_ref=st["cur"].at[tuple(give) + tail],
            dst_ref=buf,
            send_sem=send_sem.at[p, s],
            recv_sem=recv_sem.at[p, s],
            device_id=peer(k),
            device_id_type=pl.DeviceIdType.MESH,
        )
        copy.start()
        st.update(copy=copy, pos=pos, tail=tail, buf=buf)

    def end_half(p, s):
        st = state[p]
        st["copy"].wait()
        rest = len(st["left"]) - 1
        k = st["order"][s]
        for flat in range(1 << rest):
            bits = [(flat >> (rest - 1 - i)) & 1 for i in range(rest)]
            src = bits[: st["pos"]] + [bit_of(k)] + bits[st["pos"] :]
            mine = st["cur"][tuple(src) + st["tail"]].astype(F32)
            dst = tuple(bits) + (slice(None), slice(None))
            st["buf"][dst] = (mine + st["buf"][dst].astype(F32)).astype(BF16)
        st["left"].remove(k)
        st.update(cur=st["buf"], own=False)

    for p in range(nplan):
        start_half(p, 0)
    for s in range(nbits):
        for p in range(nplan):
            end_half(p, s)
            if s + 1 < nbits:
                start_half(p, s + 1)

    def held(p, s):
        fixed = state[p]["order"][: s + 1]
        lead = [bit_of(k) if k in fixed else slice(None) for k in range(nbits)[::-1]]
        return tuple(lead) + (slice(None), pl.ds(state[p]["cols"][0], state[p]["cols"][1]))

    def start_double(p, s):
        k = state[p]["order"][s]
        where = held(p, s)
        copy = pltpu.make_async_remote_copy(
            src_ref=out.at[where],
            dst_ref=out.at[where],
            send_sem=send_sem.at[p, nbits + s],
            recv_sem=recv_sem.at[p, nbits + s],
            device_id=peer(k),
            device_id_type=pl.DeviceIdType.MESH,
        )
        copy.start()
        state[p]["copy"] = copy

    for p in range(nplan):
        first, count = state[p]["cols"]
        sl = (slice(None), pl.ds(first, count))
        error = own_in[sl].astype(F32) + state[p]["buf"][...].astype(F32) - own_out[sl].astype(F32)
        out[held(p, nbits - 1)] = error.astype(BF16)
        start_double(p, nbits - 1)
    for s in range(nbits)[::-1]:
        for p in range(nplan):
            state[p]["copy"].wait()
            if s > 0:
                start_double(p, s - 1)


def exchange(terms, own_in, own_out, nrep, nten):
    rows, dim = own_in.shape
    nbits = (nrep * nten).bit_length() - 1
    tbits = nten.bit_length() - 1
    ring = list(range(tbits)) + list(range(tbits + 1, nbits))
    near, far = ring[: tbits + 1], ring[tbits + 1 :]
    turned = near[::-1]
    orders = [
        [tbits] + near + far,
        [tbits] + turned + far,
        [tbits] + turned[:1] + far + turned[1:],
        [tbits] + near[:1] + far + near[1:],
    ]
    half = dim // len(orders)
    plans = [((i * half, half), order) for i, order in enumerate(orders)]
    view = (2,) * nbits + (rows, dim)
    scratch = [
        pltpu.VMEM((2,) * (nbits - 1 - s) + (rows, half), BF16) for _ in plans for s in range(nbits)
    ]
    scratch += [pltpu.SemaphoreType.DMA((len(plans), 2 * nbits))] * 2
    vmem = pl.BlockSpec(memory_space=pltpu.VMEM)
    out = pl.pallas_call(
        functools.partial(exchange_kernel, plans, nrep, nten),
        out_shape=jax.ShapeDtypeStruct(view, BF16),
        in_specs=[vmem] * 3,
        out_specs=vmem,
        scratch_shapes=scratch,
        compiler_params=pltpu.CompilerParams(
            collective_id=0, has_side_effects=True, vmem_limit_bytes=62 << 20
        ),
    )(terms.reshape(view), own_in, own_out)
    return out.reshape(nrep, nten * rows, dim)


def dot_in(a, b):
    return lax.dot_general(a, b, (((1,), (1,)), ((), ())), preferred_element_type=F32)


def update_kernel(scales, partner, *refs):
    own, other = refs[:6], refs[6:12]
    x2 = refs[12]
    new_w, new_m = refs[13:16], refs[16:19]
    pre, hid, terms = refs[19:22]
    in_scale, hid_scale = scales

    def stepped(group, i, scale):
        weight, fac, side = group[i][0], group[3][0, i], group[5 if i == 2 else 4][0]
        grad = jnp.dot(fac, side, preferred_element_type=F32) * scale
        return (weight.astype(F32) - inner_rate * grad).astype(BF16).astype(F32)

    for i in range(3):
        scale = hid_scale if i == 2 else in_scale
        pair_mean = 0.5 * (stepped(own, i, scale) + stepped(other, i, scale))
        weight = own[i][0].astype(F32)
        outer_grad = weight - pair_mean
        updated = weight - outer_rate * (momentum_rate * outer_grad + outer_grad)
        new_w[i][0] = updated.astype(BF16)
        new_m[i][0] = outer_grad.astype(BF16)
    gate_pre = dot_in(new_w[0][0], x2[0]) * in_scale
    up_value = dot_in(new_w[1][0], x2[0]) * in_scale
    hidden = (gate_pre * jax.nn.sigmoid(gate_pre) * up_value).astype(BF16)
    term = lax.dot_general(
        hidden, new_w[2][0], (((0,), (0,)), ((), ())), preferred_element_type=F32
    ) * hid_scale
    pre[0, 0] = gate_pre
    pre[0, 1] = up_value
    hid[0] = hidden
    terms[0] = term.astype(BF16)


def share_of(weight, moment, fac, side, scale):
    grad = jnp.dot(fac, side, preferred_element_type=F32) * scale
    local = (weight.astype(F32) - inner_rate * grad).astype(BF16).astype(F32)
    return 0.475 * local - 0.2025 * moment.astype(F32)


def joined(weight, mine, theirs):
    return (0.05 * weight.astype(F32) + mine + theirs.astype(BF16).astype(F32)).astype(BF16)


def last_down_kernel(scales, partner, *refs):
    own, other, out = refs[:4], refs[4:8], refs[8]
    mine, theirs = (share_of(*(ref[0] for ref in group), scales[1]) for group in (own, other))
    out[0] = joined(own[0][0], mine, theirs)


def last_units_kernel(scales, partner, *refs):
    own, other, outs = refs[:8], refs[8:16], refs[16:]
    in_scale, hid_scale = scales

    def shares(group):
        down, x2, e2, pre = group[4][0], group[5][0], group[6][0], group[7]
        gate_pre, up_value = pre[0, 0], pre[0, 1]
        back = dot_in(down, e2) * hid_scale
        sig = jax.nn.sigmoid(gate_pre)
        delta_gate = (back * up_value * sig * (1.0 + gate_pre * (1.0 - sig))).astype(BF16)
        delta_up = (back * (gate_pre * sig)).astype(BF16)
        for i, fac in enumerate((delta_gate, delta_up)):
            yield share_of(group[i][0], group[2 + i][0], fac, x2, in_scale)

    for i, (mine, theirs) in enumerate(zip(shares(own), shares(other))):
        outs[i][0] = joined(own[i][0], mine, theirs)


def over_replicas(kernel, scales, partner, paired, single, out_shapes, flops):
    nrep = partner.shape[0]

    def spec(shape, swap):
        zeros = (0,) * (len(shape) - 1)
        if swap:
            return pl.BlockSpec((1,) + shape[1:], lambda p, who: (who[p],) + zeros)
        return pl.BlockSpec((1,) + shape[1:], lambda p, who: (p,) + zeros)

    args = list(paired) + list(paired) + list(single)
    swaps = [False] * len(paired) + [True] * len(paired) + [False] * len(single)
    moved = sum(a.size * a.dtype.itemsize for a in args)
    return pl.pallas_call(
        functools.partial(kernel, scales),
        grid_spec=pltpu.PrefetchScalarGridSpec(
            num_scalar_prefetch=1,
            grid=(nrep,),
            in_specs=[spec(a.shape, w) for a, w in zip(args, swaps)],
            out_specs=[spec(o.shape, False) for o in out_shapes],
        ),
        out_shape=out_shapes,
        cost_estimate=pl.CostEstimate(flops=flops, bytes_accessed=moved, transcendentals=0),
        compiler_params=pltpu.CompilerParams(vmem_limit_bytes=40 << 20),
    )(partner, *args)


def rounds_in_kernels(weights, factors, x1, e1, x2, own_in, own_out, partners, scales):
    nrep, units, dim = weights[0].shape
    nten = lax.axis_size("tensor")
    rows = x1.shape[1]
    like = jax.ShapeDtypeStruct((nrep, units, dim), BF16)
    flops = 18 * nrep * units * rows * dim
    res = over_replicas(
        update_kernel,
        scales,
        partners[0],
        list(weights) + [factors, x1, e1],
        [x2],
        [like] * 6
        + [
            jax.ShapeDtypeStruct((nrep, 2, units, rows), F32),
            jax.ShapeDtypeStruct((nrep, units, rows), BF16),
            jax.ShapeDtypeStruct((nrep, rows, dim), BF16),
        ],
        flops,
    )
    pre, hid, terms = res[6:]
    e2 = exchange(terms, own_in, own_out, nrep, nten)
    gate, up, down = res[:3]
    down_new = over_replicas(
        last_down_kernel, scales, partners[1], [down, res[5], hid, e2], [], [like], flops // 3
    )[0]
    down_new, row = lax.optimization_barrier((down_new, partners[1]))
    gate_new, up_new = over_replicas(
        last_units_kernel, scales, row, [gate, up, res[3], res[4], down, x2, e2, pre], [],
        [like] * 2, flops,
    )
    return gate_new, up_new, down_new


def slice_step(weights, inputs, own_in, own_out, in_scale, hid_scale):
    w_gate, w_up, w_down = weights
    replicas, rows, dim = inputs.shape
    gate_pre = bdot(inputs, w_gate, 2, 2) * in_scale
    up_value = bdot(inputs, w_up, 2, 2) * in_scale
    sigmoid_gate = jax.nn.sigmoid(gate_pre)
    active = gate_pre * sigmoid_gate
    hidden = (active * up_value).astype(BF16)
    terms = (bdot(hidden, w_down, 2, 1) * hid_scale).astype(BF16)
    branch = lax.psum_scatter(
        terms.reshape(replicas * rows, dim), AXES, scatter_dimension=0, tiled=True
    ).astype(F32)
    own_err = (own_in.astype(F32) + branch - own_out.astype(F32)).astype(BF16)
    errors = lax.all_gather(own_err, AXES, axis=0, tiled=True).reshape(replicas, rows, dim)
    back_grad = bdot(errors, w_down, 2, 2) * hid_scale
    delta_gate = (
        back_grad * up_value * sigmoid_gate * (1.0 + gate_pre * (1.0 - sigmoid_gate))
    ).astype(BF16)
    delta_up = (back_grad * active).astype(BF16)
    grads = (
        bdot(delta_gate, inputs, 1, 1) * in_scale,
        bdot(delta_up, inputs, 1, 1) * in_scale,
        bdot(hidden, errors, 1, 1) * hid_scale,
    )
    return tuple((w.astype(F32) - inner_rate * g).astype(BF16) for w, g in zip(weights, grads))


def first_update(weight, stepped, partner):
    other = jnp.take(stepped, partner, axis=0)
    pair_mean = 0.5 * (stepped.astype(F32) + other.astype(F32))
    outer_grad = weight.astype(F32) - pair_mean
    updated = weight.astype(F32) - outer_rate * (momentum_rate * outer_grad + outer_grad)
    return updated.astype(BF16), outer_grad.astype(BF16)


def last_update(weight, stepped, moment, partner):
    own = 0.475 * stepped.astype(F32) - 0.2025 * moment.astype(F32)
    other = jnp.take(own.astype(BF16), partner, axis=0).astype(F32)
    return (0.05 * weight.astype(F32) + own + other).astype(BF16)


def body(w_gate, w_up, w_down, pool, rows_index, partners):
    nrep, nten = lax.axis_size("replica"), lax.axis_size("tensor")
    dim, units_home = w_gate.shape[1:]
    units = units_home // nrep
    in_scale, hid_scale = dim ** (-0.5), (units_home * nten) ** (-0.5)
    rows = rows_index.shape[3]

    def spread(w):
        return lax.all_to_all(w.reshape(nrep, units, dim), "replica", 0, 0, tiled=True)

    at_home = (w_gate[0].T, w_up[0].T, w_down[0])
    weights = tuple(spread(w) for w in at_home)

    picked = rows_index[0]
    in_cols = jnp.take(pool[0], picked[:, 0], axis=0)
    out_cols = jnp.take(pool[0], picked[:, 1], axis=0)
    r, t = lax.axis_index("replica"), lax.axis_index("tensor")
    own_rows = rows // nten

    def mine(x, axis):
        return lax.dynamic_slice_in_dim(x, t * own_rows, own_rows, axis)

    both = lax.all_gather(jnp.stack([in_cols, out_cols]), "tensor", axis=3, tiled=True)
    inputs, targets = both[0], both[1]
    factors, errors = home_step(at_home, inputs[0], targets[0], in_scale, hid_scale)
    full = lax.all_gather(mine(inputs, 1), AXES, axis=0, tiled=False)
    full = full.transpose(1, 0, 2, 3).reshape(ROUNDS, nrep, rows, dim)
    all_errors = lax.all_gather(mine(errors, 0), AXES, axis=0, tiled=True).reshape(nrep, rows, dim)
    stacked = jnp.stack([f.reshape(nrep, units, rows) for f in factors], axis=1)
    weights, stacked = lax.optimization_barrier((weights, stacked))
    factors = lax.all_to_all(stacked, "replica", 0, 0, tiled=True)
    own_in, own_out = mine(inputs[1], 0), mine(targets[1], 0)

    total = nrep * nten
    if units % 16 == 0 and total & (total - 1) == 0 and total * own_in.size <= 1 << 22:
        weights = rounds_in_kernels(
            weights, factors, full[0], all_errors, full[1], own_in, own_out, partners,
            (in_scale, hid_scale),
        )
    else:
        sides = (full[0], full[0], all_errors)
        scales = (in_scale, in_scale, hid_scale)
        moments = []
        updated = []
        for i in range(3):
            grad = bdot(factors[:, i], sides[i], 2, 1) * scales[i]
            stepped = (weights[i].astype(F32) - inner_rate * grad).astype(BF16)
            pair = first_update(weights[i], stepped, partners[0])
            updated.append(pair[0])
            moments.append(pair[1])
        stepped = slice_step(tuple(updated), full[1], own_in, own_out, in_scale, hid_scale)
        weights = tuple(
            last_update(w, s, m, partners[1]) for w, s, m in zip(updated, stepped, moments)
        )

    def home(w):
        return lax.all_to_all(w, "replica", 0, 0, tiled=True).reshape(units_home, dim)

    down_home, gate, up = lax.optimization_barrier((home(weights[2]), weights[0], weights[1]))
    return (home(gate).T[None], home(up).T[None], down_home[None])


def solution(mesh):
    return jax.shard_map(
        body,
        mesh=mesh,
        in_specs=(
            P("replica", None, "tensor"),
            P("replica", None, "tensor"),
            P("replica", "tensor", None),
            P("replica", None, "tensor"),
            P("replica", None, None, None),
            P(),
        ),
        out_specs=(
            P("replica", None, "tensor"),
            P("replica", None, "tensor"),
            P("replica", "tensor", None),
        ),
        check_vma=False,
    )
```
